256 devices in a mesh: cfg: 2 (over core), blk: 4 (over y), uly: 32 (over x, z).
Axes of the slice: x: 4, y: 4, z: 8, core: 2. Of those that a mesh axis runs over, the one named last changes fastest.
Arguments:
- queries: bfloat16 [16384, 4096], P(('cfg', 'blk', 'uly')), parts along dimension 0, may hold values from -24 to 24
- key_states: bfloat16 [16384, 4096], P(('cfg', 'blk', 'uly')), parts along dimension 0, may hold values from -24 to 24
- value_states: bfloat16 [16384, 4096], P(('cfg', 'blk', 'uly')), parts along dimension 0, may hold values from -6 to 6
- tile_list: int32 [16, 12], replicated, may hold values from 0 to 15, as said below
- tile_used: int32 [16], replicated, may hold values from 1 to 12, as said below
Outputs:
- attended: bfloat16 [16384, 4096], P(('cfg', 'blk', 'uly')), parts along dimension 0
The draws below stay inside these ranges and needn't reach their ends.
There are 2 independent parts, one for each index of `cfg`. The reference program is written for one: setup_inputs(seed, part) draws one part's arguments, and reference() takes and returns one part's arrays. A program takes and returns all parts, laid end to end along the dimension named above; an argument that names none is the same for every part. Nothing has to cross between parts.
Inputs may be any that keep to these rules, and one draw needn't show every extreme that they name: `tile_list`: tiles are numbered with the temporal tile row slowest, then 2 rows along the height, then 2 along the width. The first tile_used[i] entries of row i are distinct tiles whose temporal tile row differs from that of tile i by at most one, and the first of them is tile i itself; the other entries of the row are to be ignored. `tile_used`: in every draw some tile lists all 12 tiles of its window and some tile lists only itself.
All inputs are finite; a program needn't handle non-finite values.
Results may differ from the reference program's by a relative error of at most 0.0047.
Values may be sent and summed in bfloat16 or wider, within the bound.
No kernel may reach another device: no remote copies, remote signals or barrier semaphores. Data moves between devices by JAX's collectives and lax.ppermute only.
A program may use at most 64 MiB of HBM per device.

```python
import jax
import jax.numpy as jnp
from jax import lax

HEADS = 32
HD = 128
TILE = 512
TH = 2
TW = 2
SLAB = 2048
TOKENS = 8192
TILES = 16
SPAN = 12


def drawn_pair(key):
    grid_shape = (TOKENS // TILE, TILE, HEADS, HD)
    query_draw = jax.random.normal(jax.random.fold_in(key, 11), grid_shape, jnp.float32)
    key_draw = jax.random.normal(jax.random.fold_in(key, 12), grid_shape, jnp.float32)
    query_draw = jnp.clip(query_draw, -24.0, 24.0).reshape(TOKENS, HEADS * HD)
    key_draw = jnp.clip(key_draw, -24.0, 24.0).reshape(TOKENS, HEADS * HD)
    return (query_draw.astype(jnp.bfloat16), key_draw.astype(jnp.bfloat16))


def draw_queries(key, part):
    return drawn_pair(key)[0]


def draw_key_states(key, part):
    return drawn_pair(key)[1]


def tile_tables(key):
    table_key = jax.random.fold_in(key, 21)
    slab_tiles = TH * TW
    tile_ids = jnp.arange(TILES, dtype=jnp.int32)
    temporal = tile_ids // slab_tiles
    slot_ids = jnp.arange(SPAN, dtype=jnp.int32)
    candidate = (temporal[:, None] - 1) * slab_tiles + slot_ids[None, :]
    inside = (candidate >= 0) & (candidate < TILES)
    itself = candidate == tile_ids[:, None]
    priority = jax.random.randint(jax.random.fold_in(table_key, 1), (TILES, SPAN), 0, 1 << 20)
    ranking = priority * SPAN + slot_ids[None, :]
    ranking = jnp.where(itself, -1, jnp.where(inside, ranking, 1 << 30))
    ranked = jnp.argsort(ranking, axis=1, stable=True)
    safe_candidate = jnp.where(inside, candidate, tile_ids[:, None])
    listed = jnp.take_along_axis(safe_candidate, ranked, axis=1)
    window_size = jnp.sum(inside.astype(jnp.int32), axis=1)
    counts = 1 + jax.random.randint(jax.random.fold_in(table_key, 2), (TILES,), 0, 1 << 20) % window_size
    pick_full = jax.random.randint(jax.random.fold_in(table_key, 3), (), slab_tiles, TILES - slab_tiles)
    pick_one = (pick_full + 1 + jax.random.randint(jax.random.fold_in(table_key, 4), (), 0, TILES - 1)) % TILES
    counts = jnp.where(tile_ids == pick_full, SPAN, counts)
    counts = jnp.where(tile_ids == pick_one, 1, counts)
    return (listed.astype(jnp.int32), counts.astype(jnp.int32))


def draw_tile_list(key, part):
    return tile_tables(key)[0]


def draw_tile_used(key, part):
    return tile_tables(key)[1]


def shard_levels(rng, extent, cuts, low, high):
    level, own = 1.0, jax.random.fold_in(rng, 6)
    for dim, parts in cuts:
        draws = jnp.exp(jax.random.uniform(jax.random.fold_in(own, dim), (parts,), jnp.float32, low / len(cuts), high / len(cuts)))
        level = level * jnp.repeat(draws, extent[dim] // parts).reshape([-1 if axis == dim else 1 for axis in range(len(extent))])
    return level


def normal_values(stream_key, extent, deviation, reach, shards=(), kind=jnp.bfloat16):
    drawn = jax.random.normal(stream_key, extent, jnp.float32) * deviation
    if len(shards) > 0:
        drawn = shard_levels(stream_key, extent, shards, -0.22, 0.18) * drawn
    return jnp.clip(drawn, min=-reach, max=reach).astype(kind)


def setup_inputs(seed: int = 0, part: int = 0) -> dict:
    keys = jax.random.split(jax.random.key(seed), 6)
    part_splits = jax.random.split(jax.random.fold_in(keys[5], part), 6)
    queries = draw_queries(jax.random.fold_in(jax.random.fold_in(keys[5], part), 71), part)
    key_states = draw_key_states(jax.random.fold_in(jax.random.fold_in(keys[5], part), 71), part)
    value_states = normal_values(part_splits[2], (TOKENS, HEADS * HD), 1.0, 6.0, ((0, 128),))
    tile_list = draw_tile_list(jax.random.fold_in(keys[5], 71), part)
    tile_used = draw_tile_used(jax.random.fold_in(keys[5], 71), part)
    return dict(queries=queries, key_states=key_states, value_states=value_states, tile_list=tile_list, tile_used=tile_used)


MASKED_SCORE = -1.0e30


def attended_table(tile_list, tile_used):
    slot_ids = jnp.arange(tile_list.shape[1], dtype=jnp.int32)
    live = slot_ids[None, :] < tile_used[:, None]
    tile_ids = jnp.arange(tile_list.shape[0], dtype=jnp.int32)
    hits = (tile_list[:, :, None] == tile_ids[None, None, :]) & live[:, :, None]
    return jnp.any(hits, axis=1)


def head_part(packed):
    query_head, key_head, value_head, allowed = packed
    scores = jnp.dot(query_head, key_head.T, preferred_element_type=jnp.float32) * (HD ** -0.5)
    masked = jnp.where(allowed[None, :], scores, MASKED_SCORE)
    row_max = jnp.max(masked, axis=-1, keepdims=True)
    weights = jnp.where(allowed[None, :], jnp.exp(scores - row_max), jnp.float32(0.0))
    row_total = jnp.sum(weights, axis=-1, keepdims=True)
    rounded = weights.astype(jnp.bfloat16)
    weighted = jnp.dot(rounded, value_head, preferred_element_type=jnp.float32)
    return (weighted / row_total).astype(jnp.bfloat16)


def reference(queries, key_states, value_states, tile_list, tile_used):
    allowed_tiles = attended_table(tile_list, tile_used)
    slab_tiles = TH * TW
    padding = jnp.zeros((SLAB, HEADS * HD), jnp.bfloat16)
    keys_padded = jnp.concatenate([padding, key_states, padding], axis=0).reshape(-1, HEADS, HD)
    values_padded = jnp.concatenate([padding, value_states, padding], axis=0).reshape(-1, HEADS, HD)
    query_grid = queries.reshape(TILES, TILE, HEADS, HD)
    tile_ids = jnp.arange(TILES, dtype=jnp.int32)

    def one_tile(tile_index):
        slab_index = tile_index // slab_tiles
        query_tile = lax.dynamic_index_in_dim(query_grid, tile_index, 0, keepdims=False)
        window_start = (slab_index * SLAB).astype(jnp.int32)
        key_window = lax.dynamic_slice_in_dim(keys_padded, window_start, 3 * SLAB, 0)
        value_window = lax.dynamic_slice_in_dim(values_padded, window_start, 3 * SLAB, 0)
        row_tiles = (slab_index - 1) * slab_tiles + jnp.arange(3 * SLAB, dtype=jnp.int32) // TILE
        tile_row = lax.dynamic_index_in_dim(allowed_tiles, tile_index, 0, keepdims=False)
        allowed = jnp.any((row_tiles[:, None] == tile_ids[None, :]) & tile_row[None, :], axis=1)
        count_heads = jnp.broadcast_to(allowed[None, :], (HEADS, 3 * SLAB))
        result = lax.map(head_part, (jnp.transpose(query_tile, (1, 0, 2)), jnp.transpose(key_window, (1, 0, 2)), jnp.transpose(value_window, (1, 0, 2)), count_heads))
        return jnp.transpose(result, (1, 0, 2)).reshape(TILE, HEADS * HD)

    return lax.map(one_tile, tile_ids).reshape(TOKENS, HEADS * HD)
```

```python
import math

import jax
import jax.numpy as jnp
from jax import lax
from jax.experimental import pallas as pl
from jax.experimental.pallas import tpu as pltpu
from jax.sharding import PartitionSpec as P

HD=128; TILE=512
C = HD ** -0.5 * math.log2(math.e)
F32=jnp.float32; BF=jnp.bfloat16

def attn_kernel(tl, used, blk, q_hbm, low_hbm, own_hbm, high_hbm, o_ref, kv, qv, S, mx, acc, sems):
    b = blk[0]
    cps=[pltpu.make_async_copy(q_hbm, qv, sems.at[0]),
         pltpu.make_async_copy(low_hbm, kv.at[pl.ds(0,32)], sems.at[1]),
         pltpu.make_async_copy(own_hbm, kv.at[pl.ds(32,32)], sems.at[2]),
         pltpu.make_async_copy(high_hbm, kv.at[pl.ds(64,32)], sems.at[3])]
    for c in cps: c.start()
    for c in cps: c.wait()
    def tile(i, _):
        g = 4*b + i
        n = used[g]
        q = qv[pl.ds(8*i, 8)].reshape(TILE, HD)
        mx[...] = jnp.full(mx.shape, -3e38, F32)
        def p1(s, _):
            t = tl[g, s] - 4*b + 4
            k = kv[pl.ds(8*t, 8), 0].reshape(TILE, HD)
            sc = lax.dot_general(q, k, (((1,),(1,)),((),())), preferred_element_type=F32)
            S[s] = sc
            m = jnp.maximum(jnp.maximum(sc[:, :128], sc[:, 128:256]), jnp.maximum(sc[:, 256:384], sc[:, 384:]))
            mx[...] = jnp.maximum(mx[...], m)
            return 0
        lax.fori_loop(0, n, p1, 0)
        mx[...] = jnp.broadcast_to(jnp.max(mx[...], axis=1, keepdims=True) * C, mx.shape)
        acc[...] = jnp.zeros_like(acc)
        def p2(s, _):
            t = tl[g, s] - 4*b + 4
            v = kv[pl.ds(8*t, 8), 1].reshape(TILE, HD)
            vx = jnp.concatenate([v, jnp.ones_like(v)], axis=1)
            m = mx[...]
            p = jnp.concatenate([jnp.exp2(S[s, :, 128*j:128*(j+1)] * C - m).astype(BF) for j in range(4)], axis=1)
            acc[...] += jnp.dot(p, vx, preferred_element_type=F32)
            return 0
        lax.fori_loop(0, n, p2, 0)
        o_ref[pl.ds(8*i, 8)] = (acc[:, :128] / acc[:, 128:]).astype(BF).reshape(8, 64, HD)
        return 0
    lax.fori_loop(0, 4, tile, 0)

def attention(tl, used, blk, q, low, own, high):
    anyspec = pl.BlockSpec(memory_space=pl.ANY)
    return pl.pallas_call(
        attn_kernel,
        grid_spec=pltpu.PrefetchScalarGridSpec(
            num_scalar_prefetch=3, grid=(1,),
            in_specs=[anyspec]*4,
            out_specs=pl.BlockSpec((32,64,HD), lambda i,*_: (0,0,0)),
            scratch_shapes=[pltpu.VMEM((96,2,64,HD),BF), pltpu.VMEM((32,64,HD),BF), pltpu.VMEM((12,TILE,TILE),F32),
                            pltpu.VMEM((TILE,128),F32), pltpu.VMEM((TILE,256),F32), pltpu.SemaphoreType.DMA((4,))]),
        out_shape=jax.ShapeDtypeStruct((32,64,HD),BF),
        compiler_params=pltpu.CompilerParams(vmem_limit_bytes=48*2**20),
        cost_estimate=pl.CostEstimate(flops=32*2*2*512*512*128, bytes_accessed=4*2**20, transcendentals=32*512*512),
    )(tl, used, blk, q, low, own, high)

def heads_first(x):
    return jnp.transpose(x.reshape(x.shape[0], -1, HD), (1, 0, 2))


def exchange(x):
    return lax.all_to_all(x, "uly", split_axis=0, concat_axis=0, tiled=True)


def body(queries, key_states, value_states, tile_list, tile_used):
    blk = lax.axis_index("blk").astype(jnp.int32).reshape(1)
    count = lax.axis_size("blk")
    up = [(i, i + 1) for i in range(count - 1)]
    down = [(i + 1, i) for i in range(count - 1)]
    kv = exchange(jnp.stack([heads_first(key_states), heads_first(value_states)], axis=1))
    q = heads_first(queries)
    kv, q = lax.optimization_barrier((kv, q))
    low = lax.ppermute(kv, "blk", up)
    high = lax.ppermute(kv, "blk", down)
    q = exchange(q)
    out = attention(tile_list, tile_used, blk, q, low, kv, high)
    out = exchange(out)
    return jnp.transpose(out, (1, 0, 2)).reshape(queries.shape)


def solution(mesh):
    spec = P(("cfg", "blk", "uly"), None)
    return jax.shard_map(
        body,
        mesh=mesh,
        in_specs=(spec, spec, spec, P(), P()),
        out_specs=spec,
        check_vma=False,
    )
```

```python
import math

import jax
import jax.numpy as jnp
from jax import lax
from jax.experimental import pallas as pl
from jax.experimental.pallas import tpu as pltpu
from jax.sharding import PartitionSpec as P

HD=128; TILE=512
U=4
GROUP=2
SLOTS=12*GROUP+U
C = HD ** -0.5 * math.log2(math.e)
F32=jnp.float32; BF=jnp.bfloat16

def attn_kernel(tl, used, blk, q_hbm, low_hbm, own_hbm, high_hbm, o_ref, kv, qv, S, mx, acc, it, iq, ia, sems):
    b = blk[0]
    regions = (low_hbm, own_hbm, high_hbm)
    q_copy = pltpu.make_async_copy(q_hbm, qv, sems.at[0])
    k_copies = [pltpu.make_async_copy(r.at[:, 0], kv.at[0, pl.ds(32*j, 32)], sems.at[1+j]) for j, r in enumerate(regions)]
    v_copies = [pltpu.make_async_copy(r.at[:, 1], kv.at[1, pl.ds(32*j, 32)], sems.at[4+j]) for j, r in enumerate(regions)]
    for c in [q_copy] + k_copies + v_copies:
        c.start()
    for grp in range(4//GROUP):
        f = jnp.int32(0)
        for a in range(GROUP):
            g = 4*b + grp*GROUP + a
            def put(s, f):
                it[f] = tl[g, s] - 4*b + 4
                iq[f] = jnp.int32(grp*GROUP + a)
                ia[f] = jnp.int32(a)
                return f + 1
            f = lax.fori_loop(0, used[g], put, f)
        for j in range(U-1):
            it[f+j] = jnp.int32(4)
            iq[f+j] = jnp.int32(0)
            ia[f+j] = jnp.int32(GROUP)
        trips = (f + (U-1)) // U
        mx[...] = jnp.full(mx.shape, -3e38, F32)
        acc[...] = jnp.zeros_like(acc)
        def p1(c, _):
            for j in range(U):
                s = c*U + j
                q = qv[pl.ds(8*iq[s], 8)].reshape(TILE, HD)
                k = kv[0, pl.ds(8*it[s], 8)].reshape(TILE, HD)
                sc = lax.dot_general(q, k, (((1,),(1,)),((),())), preferred_element_type=F32)
                S[s] = sc
                m = jnp.maximum(jnp.maximum(sc[:, :128], sc[:, 128:256]), jnp.maximum(sc[:, 256:384], sc[:, 384:]))
                mx[ia[s]] = jnp.maximum(mx[ia[s]], m)
            return 0
        if grp == 0:
            for c in [q_copy] + k_copies:
                c.wait()
        lax.fori_loop(0, trips, p1, 0)
        for a in range(GROUP):
            mx[a] = jnp.broadcast_to(jnp.max(mx[a], axis=1, keepdims=True) * C, (TILE,128))
        def p2(c, _):
            for j in range(U):
                s = c*U + j
                v = kv[1, pl.ds(8*it[s], 8)].reshape(TILE, HD)
                vx = jnp.concatenate([v, jnp.ones_like(v)], axis=1)
                m = mx[ia[s]]
                p = jnp.concatenate([jnp.exp2(S[s, :, 128*j:128*(j+1)] * C - m).astype(BF) for j in range(4)], axis=1)
                acc[ia[s]] += jnp.dot(p, vx, preferred_element_type=F32)
            return 0
        if grp == 0:
            for c in v_copies:
                c.wait()
        lax.fori_loop(0, trips, p2, 0)
        for a in range(GROUP):
            i = grp*GROUP + a
            o_ref[pl.ds(8*i, 8)] = (acc[a, :, :128] / acc[a, :, 128:]).astype(BF).reshape(8, 64, HD)

def attention(tl, used, blk, q, low, own, high):
    anyspec = pl.BlockSpec(memory_space=pl.ANY)
    return pl.pallas_call(
        attn_kernel,
        grid_spec=pltpu.PrefetchScalarGridSpec(
            num_scalar_prefetch=3, grid=(1,),
            in_specs=[anyspec]*4,
            out_specs=pl.BlockSpec((32,64,HD), lambda i,*_: (0,0,0)),
            scratch_shapes=[pltpu.VMEM((2,96,64,HD),BF), pltpu.VMEM((32,64,HD),BF), pltpu.VMEM((SLOTS,TILE,TILE),F32),
                            pltpu.VMEM((GROUP+1,TILE,128),F32), pltpu.VMEM((GROUP+1,TILE,256),F32),
                            pltpu.SMEM((SLOTS,),jnp.int32),pltpu.SMEM((SLOTS,),jnp.int32),pltpu.SMEM((SLOTS,),jnp.int32),
                            pltpu.SemaphoreType.DMA((7,))]),
        out_shape=jax.ShapeDtypeStruct((32,64,HD),BF),
        compiler_params=pltpu.CompilerParams(vmem_limit_bytes=38*2**20),
        cost_estimate=pl.CostEstimate(flops=32*2*2*512*512*128, bytes_accessed=4*2**20, transcendentals=32*512*512),
    )(tl, used, blk, q, low, own, high)

def pack_kernel(*refs):
    ins, out = refs[:-1], refs[-1]
    for h in range(out.shape[0]):
        for a, r in enumerate(ins):
            piece = r[:, HD * h : HD * (h + 1)]
            if len(ins) > 1:
                out[h, a] = piece
            else:
                out[h] = piece


def pack(*arrays):
    rows, width = arrays[0].shape
    heads = width // HD
    steps = 2
    inner = (len(arrays), rows, HD) if len(arrays) > 1 else (rows, HD)
    nbytes = 2 * len(arrays) * rows * width * 2
    return pl.pallas_call(
        pack_kernel,
        grid=(steps,),
        in_specs=[pl.BlockSpec((rows, width // steps), lambda i: (0, i))] * len(arrays),
        out_specs=pl.BlockSpec((heads // steps,) + inner, lambda i: (i,) + (0,) * len(inner)),
        out_shape=jax.ShapeDtypeStruct((heads,) + inner, arrays[0].dtype),
        cost_estimate=pl.CostEstimate(flops=0, bytes_accessed=nbytes, transcendentals=0),
    )(*arrays)


def exchange(x):
    return lax.all_to_all(x, "uly", split_axis=0, concat_axis=0, tiled=True)


def body(queries, key_states, value_states, tile_list, tile_used):
    blk = lax.axis_index("blk").astype(jnp.int32).reshape(1)
    count = lax.axis_size("blk")
    up = [(i, (i + 1) % count) for i in range(count)]
    down = [((i + 1) % count, i) for i in range(count)]
    kv = exchange(pack(key_states, value_states))
    q = pack(queries)
    kv, q = lax.optimization_barrier((kv, q))
    low = lax.ppermute(kv, "blk", up)
    high = lax.ppermute(kv, "blk", down)
    q = exchange(q)
    out = attention(tile_list, tile_used, blk, q, low, kv, high)
    out = exchange(out)
    return jnp.transpose(out, (1, 0, 2)).reshape(queries.shape)


def solution(mesh):
    spec = P(("cfg", "blk", "uly"), None)
    return jax.shard_map(
        body,
        mesh=mesh,
        in_specs=(spec, spec, spec, P(), P()),
        out_specs=spec,
        check_vma=False,
    )
```

```python
import math

import jax
import jax.numpy as jnp
from jax import lax
from jax.experimental import pallas as pl
from jax.experimental.pallas import tpu as pltpu
from jax.sharding import PartitionSpec as P

HD = 128
TILE = 512
TILES_HERE = 4
SPAN = 12
STEP = 4
SLOTS = 36
LOG2_SCALE = HD ** -0.5 * math.log2(math.e)


def plan_kernel(tile_list, tile_used, blk, key_tile, row_tile, trips):
    first = blk[0] * TILES_HERE
    total = tile_used[first]
    for i in range(1, TILES_HERE):
        total = total + tile_used[first + i]
    split = total > SLOTS

    def add(i, group, filled):
        def put(s, filled):
            key_tile[group, filled] = tile_list[first + i, s] - first + TILES_HERE
            row_tile[group, filled] = jnp.int32(i)
            return filled + 1

        return lax.fori_loop(0, tile_used[first + i], put, filled)

    def close(group, filled):
        for j in range(STEP - 1):
            key_tile[group, filled + j] = jnp.int32(TILES_HERE)
            row_tile[group, filled + j] = jnp.int32(TILES_HERE)
        trips[group] = (filled + (STEP - 1)) // STEP

    filled = jnp.int32(0)
    for i in range(TILES_HERE - 1):
        filled = add(i, 0, filled)
    last_group = split.astype(jnp.int32)
    start = jnp.where(split, 0, filled)
    close(0, filled)
    trips[1] = jnp.int32(0)
    ended = add(TILES_HERE - 1, last_group, start)
    close(last_group, ended)
    trips[2] = last_group + 1


def plan(tile_list, tile_used, blk):
    smem = pl.BlockSpec(memory_space=pltpu.SMEM)
    width = SLOTS + STEP
    return pl.pallas_call(
        plan_kernel,
        in_specs=[smem] * 3,
        out_specs=[smem] * 3,
        out_shape=[
            jax.ShapeDtypeStruct((2, width), jnp.int32),
            jax.ShapeDtypeStruct((2, width), jnp.int32),
            jax.ShapeDtypeStruct((3,), jnp.int32),
        ],
    )(tile_list, tile_used, blk)


def attention_kernel(
    key_tile, row_tile, trips, q_in, low_in, own_in, high_in, out, q_all, kv, scores, tops, sums, sems
):
    near = (own_in, low_in, high_in)
    place = (1, 0, 2)
    third = kv.shape[1] // 3
    first_copies = [pltpu.make_async_copy(q_in, q_all, sems.at[0])]
    later_copies = []
    for j in range(3):
        span = pl.ds(third * place[j], third)
        first_copies.append(pltpu.make_async_copy(near[j].at[:, 0], kv.at[0, span], sems.at[1 + j]))
        later_copies.append(pltpu.make_async_copy(near[j].at[:, 1], kv.at[1, span], sems.at[4 + j]))
    for c in first_copies + later_copies:
        c.start()
    tops[...] = jnp.full(tops.shape, -3e38, jnp.float32)
    sums[...] = jnp.zeros_like(sums)
    for c in first_copies:
        c.wait()

    def group(g, _):
        def score(step, _):
            for j in range(STEP):
                s = step * STEP + j
                row = row_tile[g, s]
                q = q_all[pl.ds(8 * jnp.minimum(row, TILES_HERE - 1), 8)].reshape(TILE, HD)
                k = kv[0, pl.ds(8 * key_tile[g, s], 8)].reshape(TILE, HD)
                dots = lax.dot_general(
                    q, k, (((1,), (1,)), ((), ())), preferred_element_type=jnp.float32
                )
                scores[s] = dots
                lanes = [dots[:, HD * n : HD * (n + 1)] for n in range(TILE // HD)]
                top = jnp.maximum(jnp.maximum(lanes[0], lanes[1]), jnp.maximum(lanes[2], lanes[3]))
                tops[row] = jnp.maximum(tops[row], top)
            return 0

        lax.fori_loop(0, trips[g], score, 0)

        @pl.when(g == 0)
        def _():
            for c in later_copies:
                c.wait()

        for i in range(TILES_HERE):
            top = jnp.max(tops[i], axis=1, keepdims=True) * LOG2_SCALE
            tops[i] = jnp.broadcast_to(top, (TILE, HD))

        def weigh(step, _):
            for j in range(STEP):
                s = step * STEP + j
                row = row_tile[g, s]
                v = kv[1, pl.ds(8 * key_tile[g, s], 8)].reshape(TILE, HD)
                v = jnp.concatenate([v, jnp.ones_like(v)], axis=1)
                top = tops[row]
                weights = [
                    jnp.exp2(scores[s, :, HD * n : HD * (n + 1)] * LOG2_SCALE - top)
                    for n in range(TILE // HD)
                ]
                weights = jnp.concatenate([w.astype(jnp.bfloat16) for w in weights], axis=1)
                sums[row] += jnp.dot(weights, v, preferred_element_type=jnp.float32)
            return 0

        lax.fori_loop(0, trips[g], weigh, 0)
        return 0

    lax.fori_loop(0, trips[2], group, 0)
    for i in range(TILES_HERE):
        result = sums[i, :, :HD] / sums[i, :, HD:]
        out[pl.ds(8 * i, 8)] = result.astype(jnp.bfloat16).reshape(8, TILE // 8, HD)


def attend(planned, q, low, own, high):
    anywhere = pl.BlockSpec(memory_space=pl.ANY)
    return pl.pallas_call(
        attention_kernel,
        grid_spec=pltpu.PrefetchScalarGridSpec(
            num_scalar_prefetch=3,
            grid=(1,),
            in_specs=[anywhere] * 4,
            out_specs=pl.BlockSpec(q.shape, lambda i, *_: (0, 0, 0)),
            scratch_shapes=[
                pltpu.VMEM(q.shape, q.dtype),
                pltpu.VMEM((2, 3 * q.shape[0]) + q.shape[1:], q.dtype),
                pltpu.VMEM((SLOTS, TILE, TILE), jnp.float32),
                pltpu.VMEM((TILES_HERE + 1, TILE, HD), jnp.float32),
                pltpu.VMEM((TILES_HERE + 1, TILE, 2 * HD), jnp.float32),
                pltpu.SemaphoreType.DMA((7,)),
            ],
        ),
        out_shape=jax.ShapeDtypeStruct(q.shape, q.dtype),
        compiler_params=pltpu.CompilerParams(vmem_limit_bytes=49 * 2**20),
        cost_estimate=pl.CostEstimate(
            flops=32 * 4 * TILE * TILE * HD, bytes_accessed=4 * 2**20, transcendentals=32 * TILE * TILE
        ),
    )(*planned, q, low, own, high)


def pack_kernel(*refs):
    ins, out = refs[:-1], refs[-1]
    for h in range(out.shape[0]):
        for a, r in enumerate(ins):
            piece = r[:, HD * h : HD * (h + 1)]
            if len(ins) > 1:
                out[h, a] = piece
            else:
                out[h] = piece


def pack(*arrays):
    rows, width = arrays[0].shape
    heads = width // HD
    steps = 2
    inner = (len(arrays), rows, HD) if len(arrays) > 1 else (rows, HD)
    nbytes = 2 * len(arrays) * rows * width * 2
    return pl.pallas_call(
        pack_kernel,
        grid=(steps,),
        in_specs=[pl.BlockSpec((rows, width // steps), lambda i: (0, i))] * len(arrays),
        out_specs=pl.BlockSpec((heads // steps,) + inner, lambda i: (i,) + (0,) * len(inner)),
        out_shape=jax.ShapeDtypeStruct((heads,) + inner, arrays[0].dtype),
        cost_estimate=pl.CostEstimate(flops=0, bytes_accessed=nbytes, transcendentals=0),
    )(*arrays)


def exchange(x):
    return lax.all_to_all(x, "uly", split_axis=0, concat_axis=0, tiled=True)


def body(queries, key_states, value_states, tile_list, tile_used):
    blk = lax.axis_index("blk").astype(jnp.int32).reshape(1)
    count = lax.axis_size("blk")
    up = [(i, (i + 1) % count) for i in range(count)]
    down = [((i + 1) % count, i) for i in range(count)]
    kv = exchange(pack(key_states, value_states))
    q = pack(queries)
    planned = plan(tile_list, tile_used, blk)
    kv, q, planned = lax.optimization_barrier((kv, q, planned))
    low = lax.ppermute(kv, "blk", up)
    high = lax.ppermute(kv, "blk", down)
    q = exchange(q)
    out = attend(planned, q, low, kv, high)
    out = exchange(out)
    return jnp.transpose(out, (1, 0, 2)).reshape(queries.shape)


def solution(mesh):
    spec = P(("cfg", "blk", "uly"), None)
    return jax.shard_map(
        body,
        mesh=mesh,
        in_specs=(spec, spec, spec, P(), P()),
        out_specs=spec,
        check_vma=False,
    )
```

```python
import math

import jax
import jax.numpy as jnp
from jax import lax
from jax.experimental import pallas as pl
from jax.experimental.pallas import tpu as pltpu
from jax.sharding import PartitionSpec as P

HD = 128
TILE = 512
TILES_HERE = 4
SPAN = 12
STEP = 4
SLOTS = 36
LOG2_SCALE = HD ** -0.5 * math.log2(math.e)


def plan_kernel(tile_list, tile_used, blk, key_tile, row_tile, trips):
    first = blk[0] * TILES_HERE
    total = tile_used[first]
    for i in range(1, TILES_HERE):
        total = total + tile_used[first + i]
    split = total > SLOTS

    def add(i, group, filled):
        def put(s, filled):
            key_tile[group, filled] = tile_list[first + i, s] - first + TILES_HERE
            row_tile[group, filled] = jnp.int32(i)
            return filled + 1

        return lax.fori_loop(0, tile_used[first + i], put, filled)

    def close(group, filled):
        for j in range(STEP - 1):
            key_tile[group, filled + j] = jnp.int32(TILES_HERE)
            row_tile[group, filled + j] = jnp.int32(TILES_HERE)
        trips[group] = (filled + (STEP - 1)) // STEP

    filled = jnp.int32(0)
    for i in range(TILES_HERE - 1):
        filled = add(i, 0, filled)
    last_group = split.astype(jnp.int32)
    start = jnp.where(split, 0, filled)
    close(0, filled)
    trips[1] = jnp.int32(0)
    ended = add(TILES_HERE - 1, last_group, start)
    close(last_group, ended)
    trips[2] = last_group + 1


def plan(tile_list, tile_used, blk):
    smem = pl.BlockSpec(memory_space=pltpu.SMEM)
    width = SLOTS + STEP
    return pl.pallas_call(
        plan_kernel,
        in_specs=[smem] * 3,
        out_specs=[smem] * 3,
        out_shape=[
            jax.ShapeDtypeStruct((2, width), jnp.int32),
            jax.ShapeDtypeStruct((2, width), jnp.int32),
            jax.ShapeDtypeStruct((3,), jnp.int32),
        ],
    )(tile_list, tile_used, blk)


def attention_kernel(
    key_tile, row_tile, trips, q_in, low_in, own_in, high_in, out, q_all, kv, scores, tops, sums, sems
):
    near = (own_in, low_in, high_in)
    place = (1, 0, 2)
    third = kv.shape[1] // 3
    first_copies = [pltpu.make_async_copy(q_in, q_all, sems.at[0])]
    later_copies = []
    for j in range(3):
        span = pl.ds(third * place[j], third)
        first_copies.append(pltpu.make_async_copy(near[j].at[:, 0], kv.at[0, span], sems.at[1 + j]))
        later_copies.append(pltpu.make_async_copy(near[j].at[:, 1], kv.at[1, span], sems.at[4 + j]))
    for c in first_copies + later_copies:
        c.start()
    tops[...] = jnp.full(tops.shape, -3e38, jnp.float32)
    sums[...] = jnp.zeros_like(sums)
    for c in first_copies:
        c.wait()

    def group(g, _):
        def score(step, _):
            for j in range(STEP):
                s = step * STEP + j
                row = row_tile[g, s]
                q = q_all[pl.ds(8 * jnp.minimum(row, TILES_HERE - 1), 8)].reshape(TILE, HD)
                k = kv[0, pl.ds(8 * key_tile[g, s], 8)].reshape(TILE, HD)
                dots = lax.dot_general(
                    q, k, (((1,), (1,)), ((), ())), preferred_element_type=jnp.float32
                )
                scores[s] = dots
                lanes = [dots[:, HD * n : HD * (n + 1)] for n in range(TILE // HD)]
                top = jnp.maximum(jnp.maximum(lanes[0], lanes[1]), jnp.maximum(lanes[2], lanes[3]))
                tops[row] = jnp.maximum(tops[row], top)
            return 0

        lax.fori_loop(0, trips[g], score, 0)

        @pl.when(g == 0)
        def _():
            for c in later_copies:
                c.wait()

        for i in range(TILES_HERE):
            top = jnp.max(tops[i], axis=1, keepdims=True) * LOG2_SCALE
            tops[i] = jnp.broadcast_to(top, (TILE, HD))

        def weigh(step, _):
            for j in range(STEP):
                s = step * STEP + j
                row = row_tile[g, s]
                v = kv[1, pl.ds(8 * key_tile[g, s], 8)].reshape(TILE, HD)
                v = jnp.concatenate([v, jnp.ones_like(v)], axis=1)
                top = tops[row]
                weights = [
                    jnp.exp2(scores[s, :, HD * n : HD * (n + 1)] * LOG2_SCALE - top)
                    for n in range(TILE // HD)
                ]
                weights = jnp.concatenate([w.astype(jnp.bfloat16) for w in weights], axis=1)
                sums[row] += jnp.dot(weights, v, preferred_element_type=jnp.float32)
            return 0

        lax.fori_loop(0, trips[g], weigh, 0)
        return 0

    lax.fori_loop(0, trips[2], group, 0)
    for i in range(TILES_HERE):
        result = sums[i, :, :HD] / sums[i, :, HD:]
        out[pl.ds(8 * i, 8)] = result.astype(jnp.bfloat16).reshape(8, TILE // 8, HD)


def attend(planned, q, low, own, high):
    anywhere = pl.BlockSpec(memory_space=pl.ANY)
    return pl.pallas_call(
        attention_kernel,
        grid_spec=pltpu.PrefetchScalarGridSpec(
            num_scalar_prefetch=3,
            grid=(1,),
            in_specs=[anywhere] * 4,
            out_specs=pl.BlockSpec(q.shape, lambda i, *_: (0, 0, 0)),
            scratch_shapes=[
                pltpu.VMEM(q.shape, q.dtype),
                pltpu.VMEM((2, 3 * q.shape[0]) + q.shape[1:], q.dtype),
                pltpu.VMEM((SLOTS, TILE, TILE), jnp.float32),
                pltpu.VMEM((TILES_HERE + 1, TILE, HD), jnp.float32),
                pltpu.VMEM((TILES_HERE + 1, TILE, 2 * HD), jnp.float32),
                pltpu.SemaphoreType.DMA((7,)),
            ],
        ),
        out_shape=jax.ShapeDtypeStruct(q.shape, q.dtype),
        compiler_params=pltpu.CompilerParams(vmem_limit_bytes=49 * 2**20),
        cost_estimate=pl.CostEstimate(
            flops=32 * 4 * TILE * TILE * HD, bytes_accessed=4 * 2**20, transcendentals=32 * TILE * TILE
        ),
    )(*planned, q, low, own, high)


def pack_kernel(*refs):
    out = refs[-1]
    ins = refs[:out.shape[1]] if len(out.shape) == 4 else refs[:1]
    for h in range(out.shape[0]):
        for a, r in enumerate(ins):
            piece = r[:, HD * h : HD * (h + 1)]
            if len(ins) > 1:
                out[h, a] = piece
            else:
                out[h] = piece


def pack(*arrays, after=None):
    rows, width = arrays[0].shape
    heads = width // HD
    steps = 2
    inner = (len(arrays), rows, HD) if len(arrays) > 1 else (rows, HD)
    nbytes = 2 * len(arrays) * rows * width * 2
    return pl.pallas_call(
        pack_kernel,
        grid=(steps,),
        in_specs=[pl.BlockSpec((rows, width // steps), lambda i: (0, i))] * len(arrays)
        + [pl.BlockSpec(memory_space=pltpu.VMEM)] * (after is not None),
        out_specs=pl.BlockSpec((heads // steps,) + inner, lambda i: (i,) + (0,) * len(inner)),
        out_shape=jax.ShapeDtypeStruct((heads,) + inner, arrays[0].dtype),
        cost_estimate=pl.CostEstimate(flops=0, bytes_accessed=nbytes, transcendentals=0),
    )(*arrays, *([] if after is None else [after]))


def second_core():
    half = lax.axis_size("blk") * lax.axis_size("uly")
    return [(half + i, half + (i ^ 1)) for i in range(half)]


def exchange(x):
    return lax.all_to_all(x, "uly", split_axis=0, concat_axis=0, tiled=True)


def body(queries, key_states, value_states, tile_list, tile_used):
    blk = lax.axis_index("blk").astype(jnp.int32).reshape(1)
    count = lax.axis_size("blk")
    up = [(i, (i + 1) % count) for i in range(count)]
    down = [((i + 1) % count, i) for i in range(count)]
    turn = tile_used
    for _ in range(3):
        turn = lax.ppermute(turn, ("cfg", "blk", "uly"), second_core())
    kv = exchange(pack(key_states, value_states, after=turn))
    q = pack(queries)
    planned = plan(tile_list, tile_used, blk)
    kv, q, planned = lax.optimization_barrier((kv, q, planned))
    low = lax.ppermute(kv, "blk", up)
    high = lax.ppermute(kv, "blk", down)
    q = exchange(q)
    out = attend(planned, q, low, kv, high)
    out = exchange(out)
    return jnp.transpose(out, (1, 0, 2)).reshape(queries.shape)


def solution(mesh):
    spec = P(("cfg", "blk", "uly"), None)
    return jax.shard_map(
        body,
        mesh=mesh,
        in_specs=(spec, spec, spec, P(), P()),
        out_specs=spec,
        check_vma=False,
    )
```

```python
import math

import jax
import jax.numpy as jnp
from jax import lax
from jax.experimental import pallas as pl
from jax.experimental.pallas import tpu as pltpu
from jax.sharding import PartitionSpec as P

HD = 128
TILE = 512
TILES_HERE = 4
SPAN = 12
STEP = 4
SLOTS = 36
LOG2_SCALE = HD ** -0.5 * math.log2(math.e)


def plan_kernel(tile_list, tile_used, blk, key_tile, row_tile, trips):
    first = blk[0] * TILES_HERE
    total = tile_used[first]
    for i in range(1, TILES_HERE):
        total = total + tile_used[first + i]
    split = total > SLOTS

    def add(i, group, filled):
        def put(s, filled):
            key_tile[group, filled] = tile_list[first + i, s] - first + TILES_HERE
            row_tile[group, filled] = jnp.int32(i)
            return filled + 1

        return lax.fori_loop(0, tile_used[first + i], put, filled)

    def close(group, filled):
        for j in range(STEP - 1):
            key_tile[group, filled + j] = jnp.int32(TILES_HERE)
            row_tile[group, filled + j] = jnp.int32(TILES_HERE)
        trips[group] = (filled + (STEP - 1)) // STEP

    filled = jnp.int32(0)
    for i in range(TILES_HERE - 1):
        filled = add(i, 0, filled)
    last_group = split.astype(jnp.int32)
    start = jnp.where(split, 0, filled)
    close(0, filled)
    trips[1] = jnp.int32(0)
    ended = add(TILES_HERE - 1, last_group, start)
    close(last_group, ended)
    trips[2] = last_group + 1


def plan(tile_list, tile_used, blk):
    smem = pl.BlockSpec(memory_space=pltpu.SMEM)
    width = SLOTS + STEP
    return pl.pallas_call(
        plan_kernel,
        in_specs=[smem] * 3,
        out_specs=[smem] * 3,
        out_shape=[
            jax.ShapeDtypeStruct((2, width), jnp.int32),
            jax.ShapeDtypeStruct((2, width), jnp.int32),
            jax.ShapeDtypeStruct((3,), jnp.int32),
        ],
    )(tile_list, tile_used, blk)


def attention_kernel(
    key_tile, row_tile, trips, q_in, low_in, own_in, high_in, out, q_all, kv, scores, tops, sums, sems
):
    near = (own_in, low_in, high_in)
    place = (1, 0, 2)
    third = kv.shape[1] // 3
    first_copies = [pltpu.make_async_copy(q_in, q_all, sems.at[0])]
    later_copies = []
    for j in range(3):
        span = pl.ds(third * place[j], third)
        first_copies.append(pltpu.make_async_copy(near[j].at[:, 0], kv.at[0, span], sems.at[1 + j]))
        later_copies.append(pltpu.make_async_copy(near[j].at[:, 1], kv.at[1, span], sems.at[4 + j]))
    for c in first_copies + later_copies:
        c.start()
    tops[...] = jnp.full(tops.shape, -3e38, jnp.float32)
    sums[...] = jnp.zeros_like(sums)
    for c in first_copies:
        c.wait()

    def group(g, _):
        def score(step, _):
            for j in range(STEP):
                s = step * STEP + j
                row = row_tile[g, s]
                q = q_all[pl.ds(8 * jnp.minimum(row, TILES_HERE - 1), 8)].reshape(TILE, HD)
                k = kv[0, pl.ds(8 * key_tile[g, s], 8)].reshape(TILE, HD)
                dots = lax.dot_general(
                    q, k, (((1,), (1,)), ((), ())), preferred_element_type=jnp.float32
                )
                scores[s] = dots
                lanes = [dots[:, HD * n : HD * (n + 1)] for n in range(TILE // HD)]
                top = jnp.maximum(jnp.maximum(lanes[0], lanes[1]), jnp.maximum(lanes[2], lanes[3]))
                tops[row] = jnp.maximum(tops[row], top)
            return 0

        lax.fori_loop(0, trips[g], score, 0)

        @pl.when(g == 0)
        def _():
            for c in later_copies:
                c.wait()

        for i in range(TILES_HERE):
            top = jnp.max(tops[i], axis=1, keepdims=True) * LOG2_SCALE
            tops[i] = jnp.broadcast_to(top, (TILE, HD))

        def weigh(step, _):
            for j in range(STEP):
                s = step * STEP + j
                row = row_tile[g, s]
                v = kv[1, pl.ds(8 * key_tile[g, s], 8)].reshape(TILE, HD)
                v = jnp.concatenate([v, jnp.ones_like(v)], axis=1)
                top = tops[row]
                weights = [
                    jnp.exp2(scores[s, :, HD * n : HD * (n + 1)] * LOG2_SCALE - top)
                    for n in range(TILE // HD)
                ]
                weights = jnp.concatenate([w.astype(jnp.bfloat16) for w in weights], axis=1)
                sums[row] += jnp.dot(weights, v, preferred_element_type=jnp.float32)
            return 0

        lax.fori_loop(0, trips[g], weigh, 0)
        return 0

    lax.fori_loop(0, trips[2], group, 0)
    for i in range(TILES_HERE):
        result = sums[i, :, :HD] / sums[i, :, HD:]
        out[pl.ds(8 * i, 8)] = result.astype(jnp.bfloat16).reshape(8, TILE // 8, HD)


def attend(planned, q, low, own, high):
    anywhere = pl.BlockSpec(memory_space=pl.ANY)
    return pl.pallas_call(
        attention_kernel,
        grid_spec=pltpu.PrefetchScalarGridSpec(
            num_scalar_prefetch=3,
            grid=(1,),
            in_specs=[anywhere] * 4,
            out_specs=pl.BlockSpec(q.shape, lambda i, *_: (0, 0, 0)),
            scratch_shapes=[
                pltpu.VMEM(q.shape, q.dtype),
                pltpu.VMEM((2, 3 * q.shape[0]) + q.shape[1:], q.dtype),
                pltpu.VMEM((SLOTS, TILE, TILE), jnp.float32),
                pltpu.VMEM((TILES_HERE + 1, TILE, HD), jnp.float32),
                pltpu.VMEM((TILES_HERE + 1, TILE, 2 * HD), jnp.float32),
                pltpu.SemaphoreType.DMA((7,)),
            ],
        ),
        out_shape=jax.ShapeDtypeStruct(q.shape, q.dtype),
        compiler_params=pltpu.CompilerParams(vmem_limit_bytes=49 * 2**20),
        cost_estimate=pl.CostEstimate(
            flops=32 * 4 * TILE * TILE * HD, bytes_accessed=4 * 2**20, transcendentals=32 * TILE * TILE
        ),
    )(*planned, q, low, own, high)


def pack_kernel(*refs):
    out = refs[-1]
    ins = refs[:out.shape[1]] if len(out.shape) == 4 else refs[:1]
    for h in range(out.shape[0]):
        for a, r in enumerate(ins):
            piece = r[:, HD * h : HD * (h + 1)]
            if len(ins) > 1:
                out[h, a] = piece
            else:
                out[h] = piece


def pack(*arrays, after=None):
    rows, width = arrays[0].shape
    heads = width // HD
    steps = 2
    inner = (len(arrays), rows, HD) if len(arrays) > 1 else (rows, HD)
    nbytes = 2 * len(arrays) * rows * width * 2
    return pl.pallas_call(
        pack_kernel,
        grid=(steps,),
        in_specs=[pl.BlockSpec((rows, width // steps), lambda i: (0, i))] * len(arrays)
        + [pl.BlockSpec(memory_space=pltpu.VMEM)] * (after is not None),
        out_specs=pl.BlockSpec((heads // steps,) + inner, lambda i: (i,) + (0,) * len(inner)),
        out_shape=jax.ShapeDtypeStruct((heads,) + inner, arrays[0].dtype),
        cost_estimate=pl.CostEstimate(flops=0, bytes_accessed=nbytes, transcendentals=0),
    )(*arrays, *([] if after is None else [after]))


def second_cores_turn(token, along):
    uly = lax.axis_size("uly")
    half = lax.axis_size("blk") * uly
    apart = half // 2 + uly // 2 + along // 2
    pairs = [(half + i, half + (i ^ apart)) for i in range(half)]
    return lax.ppermute(token, ("cfg", "blk", "uly"), pairs)


def exchange(x):
    return lax.all_to_all(x, "uly", split_axis=0, concat_axis=0, tiled=True)


def body(queries, key_states, value_states, tile_list, tile_used):
    blk = lax.axis_index("blk").astype(jnp.int32).reshape(1)
    count = lax.axis_size("blk")
    up = [(i, (i + 1) % count) for i in range(count)]
    down = [((i + 1) % count, i) for i in range(count)]
    turn = second_cores_turn(tile_used, TILE // queries.shape[0])
    kv = exchange(pack(key_states, value_states, after=turn))
    q = pack(queries)
    planned = plan(tile_list, tile_used, blk)
    kv, q, planned = lax.optimization_barrier((kv, q, planned))
    low = lax.ppermute(kv, "blk", up)
    high = lax.ppermute(kv, "blk", down)
    q = exchange(q)
    out = attend(planned, q, low, kv, high)
    out = exchange(out)
    return jnp.transpose(out, (1, 0, 2)).reshape(queries.shape)


def solution(mesh):
    spec = P(("cfg", "blk", "uly"), None)
    return jax.shard_map(
        body,
        mesh=mesh,
        in_specs=(spec, spec, spec, P(), P()),
        out_specs=spec,
        check_vma=False,
    )
```

```python
import math

import jax
import jax.numpy as jnp
from jax import lax
from jax.experimental import pallas as pl
from jax.experimental.pallas import tpu as pltpu
from jax.sharding import PartitionSpec as P

HD = 128
TILE = 512
TILES_HERE = 4
SPAN = 12
LONG = 8
STEP = 4
SLOTS = 36
LOG2_SCALE = HD ** -0.5 * math.log2(math.e)


def plan_kernel(tile_list, tile_used, blk, key_tile, row_tile, trips):
    first = blk[0] * TILES_HERE
    total = tile_used[first]
    for i in range(1, TILES_HERE):
        total = total + tile_used[first + i]
    split = total > SLOTS

    def add(i, group, filled):
        def put(s, filled):
            key_tile[group, filled] = tile_list[first + i, s] - first + TILES_HERE
            row_tile[group, filled] = jnp.int32(i)
            return filled + 1

        return lax.fori_loop(0, tile_used[first + i], put, filled)

    def close(group, filled):
        for j in range(STEP - 1):
            key_tile[group, filled + j] = jnp.int32(TILES_HERE)
            row_tile[group, filled + j] = jnp.int32(TILES_HERE)
        trips[group] = filled // LONG
        trips[3 + group] = (lax.rem(filled, LONG) + (STEP - 1)) // STEP

    filled = jnp.int32(0)
    for i in range(TILES_HERE - 1):
        filled = add(i, 0, filled)
    last_group = split.astype(jnp.int32)
    start = jnp.where(split, 0, filled)
    close(0, filled)
    trips[1] = jnp.int32(0)
    trips[4] = jnp.int32(0)
    ended = add(TILES_HERE - 1, last_group, start)
    close(last_group, ended)
    trips[2] = last_group + 1


def plan(tile_list, tile_used, blk):
    smem = pl.BlockSpec(memory_space=pltpu.SMEM)
    width = SLOTS + STEP
    return pl.pallas_call(
        plan_kernel,
        in_specs=[smem] * 3,
        out_specs=[smem] * 3,
        out_shape=[
            jax.ShapeDtypeStruct((2, width), jnp.int32),
            jax.ShapeDtypeStruct((2, width), jnp.int32),
            jax.ShapeDtypeStruct((5,), jnp.int32),
        ],
    )(tile_list, tile_used, blk)


def attention_kernel(
    key_tile, row_tile, trips, q_in, low_in, own_in, high_in, out, q_all, kv, scores, tops, sums, sems
):
    near = (own_in, low_in, high_in)
    place = (1, 0, 2)
    third = kv.shape[1] // 3
    first_copies = [pltpu.make_async_copy(q_in, q_all, sems.at[0])]
    later_copies = []
    for j in range(3):
        span = pl.ds(third * place[j], third)
        first_copies.append(pltpu.make_async_copy(near[j].at[:, 0], kv.at[0, span], sems.at[1 + j]))
        later_copies.append(pltpu.make_async_copy(near[j].at[:, 1], kv.at[1, span], sems.at[4 + j]))
    for c in first_copies + later_copies:
        c.start()
    tops[...] = jnp.full(tops.shape, -3e38, jnp.float32)
    sums[...] = jnp.zeros_like(sums)
    for c in first_copies:
        c.wait()

    def walk(g, work):
        def long(c, _):
            work(c * LONG, LONG)
            return 0

        def short(c, _):
            work(trips[g] * LONG + c * STEP, STEP)
            return 0

        lax.fori_loop(0, trips[g], long, 0)
        lax.fori_loop(0, trips[3 + g], short, 0)

    def group(g, _):
        def score(s, count):
            for j in range(count):
                here = s + j
                row = row_tile[g, here]
                q = q_all[pl.ds(8 * jnp.minimum(row, TILES_HERE - 1), 8)].reshape(TILE, HD)
                k = kv[0, pl.ds(8 * key_tile[g, here], 8)].reshape(TILE, HD)
                dots = lax.dot_general(
                    q, k, (((1,), (1,)), ((), ())), preferred_element_type=jnp.float32
                )
                scores[here] = dots
                lanes = [dots[:, HD * n : HD * (n + 1)] for n in range(TILE // HD)]
                top = jnp.maximum(jnp.maximum(lanes[0], lanes[1]), jnp.maximum(lanes[2], lanes[3]))
                tops[row] = jnp.maximum(tops[row], top)

        walk(g, score)

        @pl.when(g == 0)
        def _():
            for c in later_copies:
                c.wait()

        for i in range(TILES_HERE):
            top = jnp.max(tops[i], axis=1, keepdims=True) * LOG2_SCALE
            tops[i] = jnp.broadcast_to(top, (TILE, HD))

        def weigh(s, count):
            for j in range(count):
                here = s + j
                row = row_tile[g, here]
                v = kv[1, pl.ds(8 * key_tile[g, here], 8)].reshape(TILE, HD)
                v = jnp.concatenate([v, jnp.ones_like(v)], axis=1)
                top = tops[row]
                weights = [
                    jnp.exp2(scores[here, :, HD * n : HD * (n + 1)] * LOG2_SCALE - top)
                    for n in range(TILE // HD)
                ]
                weights = jnp.concatenate([w.astype(jnp.bfloat16) for w in weights], axis=1)
                sums[row] += jnp.dot(weights, v, preferred_element_type=jnp.float32)

        walk(g, weigh)
        return 0

    lax.fori_loop(0, trips[2], group, 0)
    for i in range(TILES_HERE):
        result = sums[i, :, :HD] / sums[i, :, HD:]
        out[pl.ds(8 * i, 8)] = result.astype(jnp.bfloat16).reshape(8, TILE // 8, HD)


def attend(planned, q, low, own, high):
    anywhere = pl.BlockSpec(memory_space=pl.ANY)
    return pl.pallas_call(
        attention_kernel,
        grid_spec=pltpu.PrefetchScalarGridSpec(
            num_scalar_prefetch=3,
            grid=(1,),
            in_specs=[anywhere] * 4,
            out_specs=pl.BlockSpec(q.shape, lambda i, *_: (0, 0, 0)),
            scratch_shapes=[
                pltpu.VMEM(q.shape, q.dtype),
                pltpu.VMEM((2, 3 * q.shape[0]) + q.shape[1:], q.dtype),
                pltpu.VMEM((SLOTS, TILE, TILE), jnp.float32),
                pltpu.VMEM((TILES_HERE + 1, TILE, HD), jnp.float32),
                pltpu.VMEM((TILES_HERE + 1, TILE, 2 * HD), jnp.float32),
                pltpu.SemaphoreType.DMA((7,)),
            ],
        ),
        out_shape=jax.ShapeDtypeStruct(q.shape, q.dtype),
        compiler_params=pltpu.CompilerParams(vmem_limit_bytes=49 * 2**20),
        cost_estimate=pl.CostEstimate(
            flops=32 * 4 * TILE * TILE * HD, bytes_accessed=4 * 2**20, transcendentals=32 * TILE * TILE
        ),
    )(*planned, q, low, own, high)


def pack_kernel(*refs):
    out = refs[-1]
    ins = refs[:out.shape[1]] if len(out.shape) == 4 else refs[:1]
    for h in range(out.shape[0]):
        for a, r in enumerate(ins):
            piece = r[:, HD * h : HD * (h + 1)]
            if len(ins) > 1:
                out[h, a] = piece
            else:
                out[h] = piece


def pack(*arrays, after=None):
    rows, width = arrays[0].shape
    heads = width // HD
    steps = 2
    inner = (len(arrays), rows, HD) if len(arrays) > 1 else (rows, HD)
    nbytes = 2 * len(arrays) * rows * width * 2
    return pl.pallas_call(
        pack_kernel,
        grid=(steps,),
        in_specs=[pl.BlockSpec((rows, width // steps), lambda i: (0, i))] * len(arrays)
        + [pl.BlockSpec(memory_space=pltpu.VMEM)] * (after is not None),
        out_specs=pl.BlockSpec((heads // steps,) + inner, lambda i: (i,) + (0,) * len(inner)),
        out_shape=jax.ShapeDtypeStruct((heads,) + inner, arrays[0].dtype),
        cost_estimate=pl.CostEstimate(flops=0, bytes_accessed=nbytes, transcendentals=0),
    )(*arrays, *([] if after is None else [after]))


def second_cores_turn(token, along):
    uly = lax.axis_size("uly")
    half = lax.axis_size("blk") * uly
    apart = half // 2 + uly // 2 + along // 2
    pairs = [(half + i, half + (i ^ apart)) for i in range(half)]
    return lax.ppermute(token, ("cfg", "blk", "uly"), pairs)


def exchange(x):
    return lax.all_to_all(x, "uly", split_axis=0, concat_axis=0, tiled=True)


def body(queries, key_states, value_states, tile_list, tile_used):
    blk = lax.axis_index("blk").astype(jnp.int32).reshape(1)
    count = lax.axis_size("blk")
    up = [(i, (i + 1) % count) for i in range(count)]
    down = [((i + 1) % count, i) for i in range(count)]
    turn = second_cores_turn(tile_used, TILE // queries.shape[0])
    kv = exchange(pack(key_states, value_states, after=turn))
    q = pack(queries)
    planned = plan(tile_list, tile_used, blk)
    kv, q, planned = lax.optimization_barrier((kv, q, planned))
    low = lax.ppermute(kv, "blk", up)
    high = lax.ppermute(kv, "blk", down)
    q = exchange(q)
    out = attend(planned, q, low, kv, high)
    out = exchange(out)
    return jnp.transpose(out, (1, 0, 2)).reshape(queries.shape)


def solution(mesh):
    spec = P(("cfg", "blk", "uly"), None)
    return jax.shard_map(
        body,
        mesh=mesh,
        in_specs=(spec, spec, spec, P(), P()),
        out_specs=spec,
        check_vma=False,
    )
```

```python
import math

import jax
import jax.numpy as jnp
from jax import lax
from jax.experimental import pallas as pl
from jax.experimental.pallas import tpu as pltpu
from jax.sharding import PartitionSpec as P

HD = 128
TILE = 512
TILES_HERE = 4
SPAN = 12
LONG = 8
STEP = 4
SLOTS = 36
LOG2_SCALE = HD ** -0.5 * math.log2(math.e)


def plan_kernel(tile_list, tile_used, blk, turn, key_tile, row_tile, trips):
    first = blk[0] * TILES_HERE
    total = tile_used[first]
    for i in range(1, TILES_HERE):
        total = total + tile_used[first + i]
    split = total > SLOTS

    def add(i, group, filled):
        def put(s, filled):
            key_tile[group, filled] = tile_list[first + i, s] - first + TILES_HERE
            row_tile[group, filled] = jnp.int32(i)
            return filled + 1

        return lax.fori_loop(0, tile_used[first + i], put, filled)

    def close(group, filled):
        for j in range(STEP - 1):
            key_tile[group, filled + j] = jnp.int32(TILES_HERE)
            row_tile[group, filled + j] = jnp.int32(TILES_HERE)
        trips[group] = filled // LONG
        trips[3 + group] = (lax.rem(filled, LONG) + (STEP - 1)) // STEP

    filled = jnp.int32(0)
    for i in range(TILES_HERE - 1):
        filled = add(i, 0, filled)
    last_group = split.astype(jnp.int32)
    start = jnp.where(split, 0, filled)
    close(0, filled)
    trips[1] = jnp.int32(0)
    trips[4] = jnp.int32(0)
    ended = add(TILES_HERE - 1, last_group, start)
    close(last_group, ended)
    trips[2] = last_group + 1


def plan(tile_list, tile_used, blk, turn):
    smem = pl.BlockSpec(memory_space=pltpu.SMEM)
    width = SLOTS + STEP
    return pl.pallas_call(
        plan_kernel,
        in_specs=[smem] * 3 + [pl.BlockSpec(memory_space=pl.ANY)],
        out_specs=[smem] * 3,
        out_shape=[
            jax.ShapeDtypeStruct((2, width), jnp.int32),
            jax.ShapeDtypeStruct((2, width), jnp.int32),
            jax.ShapeDtypeStruct((5,), jnp.int32),
        ],
    )(tile_list, tile_used, blk, turn)


def attention_kernel(
    key_tile, row_tile, trips, q_in, low_in, own_in, high_in, out, q_all, kv, scores, tops, sums, sems
):
    near = (own_in, low_in, high_in)
    place = (1, 0, 2)
    third = kv.shape[1] // 3
    first_copies = [pltpu.make_async_copy(q_in, q_all, sems.at[0])]
    later_copies = []
    for j in range(3):
        span = pl.ds(third * place[j], third)
        first_copies.append(pltpu.make_async_copy(near[j].at[:, 0], kv.at[0, span], sems.at[1 + j]))
        later_copies.append(pltpu.make_async_copy(near[j].at[:, 1], kv.at[1, span], sems.at[4 + j]))
    for c in first_copies + later_copies:
        c.start()
    tops[...] = jnp.full(tops.shape, -3e38, jnp.float32)
    sums[...] = jnp.zeros_like(sums)
    for c in first_copies:
        c.wait()

    def walk(g, work):
        def long(c, _):
            work(c * LONG, LONG)
            return 0

        def short(c, _):
            work(trips[g] * LONG + c * STEP, STEP)
            return 0

        lax.fori_loop(0, trips[g], long, 0)
        lax.fori_loop(0, trips[3 + g], short, 0)

    def group(g, _):
        def score(s, count):
            for j in range(count):
                here = s + j
                row = row_tile[g, here]
                q = q_all[pl.ds(8 * jnp.minimum(row, TILES_HERE - 1), 8)].reshape(TILE, HD)
                k = kv[0, pl.ds(8 * key_tile[g, here], 8)].reshape(TILE, HD)
                dots = lax.dot_general(
                    q, k, (((1,), (1,)), ((), ())), preferred_element_type=jnp.float32
                )
                scores[here] = dots
                lanes = [dots[:, HD * n : HD * (n + 1)] for n in range(TILE // HD)]
                top = jnp.maximum(jnp.maximum(lanes[0], lanes[1]), jnp.maximum(lanes[2], lanes[3]))
                tops[row] = jnp.maximum(tops[row], top)

        walk(g, score)

        @pl.when(g == 0)
        def _():
            for c in later_copies:
                c.wait()

        for i in range(TILES_HERE):
            top = jnp.max(tops[i], axis=1, keepdims=True) * LOG2_SCALE
            tops[i] = jnp.broadcast_to(top, (TILE, HD))

        def weigh(s, count):
            for j in range(count):
                here = s + j
                row = row_tile[g, here]
                v = kv[1, pl.ds(8 * key_tile[g, here], 8)].reshape(TILE, HD)
                v = jnp.concatenate([v, jnp.ones_like(v)], axis=1)
                top = tops[row]
                weights = [
                    jnp.exp2(scores[here, :, HD * n : HD * (n + 1)] * LOG2_SCALE - top)
                    for n in range(TILE // HD)
                ]
                weights = jnp.concatenate([w.astype(jnp.bfloat16) for w in weights], axis=1)
                sums[row] += jnp.dot(weights, v, preferred_element_type=jnp.float32)

        walk(g, weigh)
        return 0

    lax.fori_loop(0, trips[2], group, 0)
    for i in range(TILES_HERE):
        result = sums[i, :, :HD] / sums[i, :, HD:]
        out[pl.ds(8 * i, 8)] = result.astype(jnp.bfloat16).reshape(8, TILE // 8, HD)


def attend(planned, q, low, own, high):
    anywhere = pl.BlockSpec(memory_space=pl.ANY)
    return pl.pallas_call(
        attention_kernel,
        grid_spec=pltpu.PrefetchScalarGridSpec(
            num_scalar_prefetch=3,
            grid=(1,),
            in_specs=[anywhere] * 4,
            out_specs=pl.BlockSpec(q.shape, lambda i, *_: (0, 0, 0)),
            scratch_shapes=[
                pltpu.VMEM(q.shape, q.dtype),
                pltpu.VMEM((2, 3 * q.shape[0]) + q.shape[1:], q.dtype),
                pltpu.VMEM((SLOTS, TILE, TILE), jnp.float32),
                pltpu.VMEM((TILES_HERE + 1, TILE, HD), jnp.float32),
                pltpu.VMEM((TILES_HERE + 1, TILE, 2 * HD), jnp.float32),
                pltpu.SemaphoreType.DMA((7,)),
            ],
        ),
        out_shape=jax.ShapeDtypeStruct(q.shape, q.dtype),
        compiler_params=pltpu.CompilerParams(vmem_limit_bytes=49 * 2**20),
        cost_estimate=pl.CostEstimate(
            flops=32 * 4 * TILE * TILE * HD, bytes_accessed=4 * 2**20, transcendentals=32 * TILE * TILE
        ),
    )(*planned, q, low, own, high)


def pack_kernel(*refs):
    ins, out = refs[:-1], refs[-1]
    for h in range(out.shape[0]):
        for a, r in enumerate(ins):
            piece = r[:, HD * h : HD * (h + 1)]
            if len(ins) > 1:
                out[h, a] = piece
            else:
                out[h] = piece


def pack(*arrays):
    rows, width = arrays[0].shape
    heads = width // HD
    steps = 2
    inner = (len(arrays), rows, HD) if len(arrays) > 1 else (rows, HD)
    nbytes = 2 * len(arrays) * rows * width * 2
    return pl.pallas_call(
        pack_kernel,
        grid=(steps,),
        in_specs=[pl.BlockSpec((rows, width // steps), lambda i: (0, i))] * len(arrays),
        out_specs=pl.BlockSpec((heads // steps,) + inner, lambda i: (i,) + (0,) * len(inner)),
        out_shape=jax.ShapeDtypeStruct((heads,) + inner, arrays[0].dtype),
        cost_estimate=pl.CostEstimate(flops=0, bytes_accessed=nbytes, transcendentals=0),
    )(*arrays)


def second_cores_turn(token, along):
    uly = lax.axis_size("uly")
    half = lax.axis_size("blk") * uly
    apart = half // 2 + uly // 2 + along // 2
    pairs = [(half + i, half + (i ^ apart)) for i in range(half)]
    return lax.ppermute(token, ("cfg", "blk", "uly"), pairs)


def exchange(x):
    return lax.all_to_all(x, "uly", split_axis=0, concat_axis=0, tiled=True)


def body(queries, key_states, value_states, tile_list, tile_used):
    blk = lax.axis_index("blk").astype(jnp.int32).reshape(1)
    count = lax.axis_size("blk")
    up = [(i, (i + 1) % count) for i in range(count)]
    down = [((i + 1) % count, i) for i in range(count)]
    turn = second_cores_turn(tile_used, TILE // queries.shape[0])
    key_states, turn = lax.optimization_barrier((key_states, turn))
    kv = exchange(pack(key_states, value_states))
    q = pack(queries)
    planned = plan(tile_list, tile_used, blk, turn)
    kv, q, planned = lax.optimization_barrier((kv, q, planned))
    low = lax.ppermute(kv, "blk", up)
    high = lax.ppermute(kv, "blk", down)
    q = exchange(q)
    out = attend(planned, q, low, kv, high)
    out = exchange(out)
    return jnp.transpose(out, (1, 0, 2)).reshape(queries.shape)


def solution(mesh):
    spec = P(("cfg", "blk", "uly"), None)
    return jax.shard_map(
        body,
        mesh=mesh,
        in_specs=(spec, spec, spec, P(), P()),
        out_specs=spec,
        check_vma=False,
    )
```

```python
import math

import jax
import jax.numpy as jnp
from jax import lax
from jax.experimental import pallas as pl
from jax.experimental.pallas import tpu as pltpu
from jax.sharding import PartitionSpec as P

HD = 128
TILE = 512
TILES_HERE = 4
SPAN = 12
LONG = 12
STEP = 4
SLOTS = 36
LOG2_SCALE = HD ** -0.5 * math.log2(math.e)


def plan_kernel(tile_list, tile_used, blk, turn, key_tile, row_tile, trips):
    first = blk[0] * TILES_HERE
    total = tile_used[first]
    for i in range(1, TILES_HERE):
        total = total + tile_used[first + i]
    split = total > SLOTS

    def add(i, group, filled):
        def put(s, filled):
            key_tile[group, filled] = tile_list[first + i, s] - first + TILES_HERE
            row_tile[group, filled] = jnp.int32(i)
            return filled + 1

        return lax.fori_loop(0, tile_used[first + i], put, filled)

    def close(group, filled):
        for j in range(STEP - 1):
            key_tile[group, filled + j] = jnp.int32(TILES_HERE)
            row_tile[group, filled + j] = jnp.int32(TILES_HERE)
        trips[group] = filled // LONG
        trips[3 + group] = (lax.rem(filled, LONG) + (STEP - 1)) // STEP

    filled = jnp.int32(0)
    for i in range(TILES_HERE - 1):
        filled = add(i, 0, filled)
    last_group = split.astype(jnp.int32)
    start = jnp.where(split, 0, filled)
    close(0, filled)
    trips[1] = jnp.int32(0)
    trips[4] = jnp.int32(0)
    ended = add(TILES_HERE - 1, last_group, start)
    close(last_group, ended)
    trips[2] = last_group + 1


def plan(tile_list, tile_used, blk, turn):
    smem = pl.BlockSpec(memory_space=pltpu.SMEM)
    width = SLOTS + STEP
    return pl.pallas_call(
        plan_kernel,
        in_specs=[smem] * 3 + [pl.BlockSpec(memory_space=pl.ANY)],
        out_specs=[smem] * 3,
        out_shape=[
            jax.ShapeDtypeStruct((2, width), jnp.int32),
            jax.ShapeDtypeStruct((2, width), jnp.int32),
            jax.ShapeDtypeStruct((5,), jnp.int32),
        ],
    )(tile_list, tile_used, blk, turn)


def attention_kernel(
    key_tile, row_tile, trips, q_in, low_in, own_in, high_in, out, q_all, kv, scores, tops, sums, sems
):
    near = (own_in, low_in, high_in)
    place = (1, 0, 2)
    third = kv.shape[1] // 3
    first_copies = [pltpu.make_async_copy(q_in, q_all, sems.at[0])]
    later_copies = []
    for j in range(3):
        span = pl.ds(third * place[j], third)
        first_copies.append(pltpu.make_async_copy(near[j].at[:, 0], kv.at[0, span], sems.at[1 + j]))
        later_copies.append(pltpu.make_async_copy(near[j].at[:, 1], kv.at[1, span], sems.at[4 + j]))
    for c in first_copies + later_copies:
        c.start()
    tops[...] = jnp.full(tops.shape, -3e38, jnp.float32)
    sums[...] = jnp.zeros_like(sums)
    for c in first_copies:
        c.wait()

    def walk(g, work):
        def long(c, _):
            work(c * LONG, LONG)
            return 0

        def short(c, _):
            work(trips[g] * LONG + c * STEP, STEP)
            return 0

        lax.fori_loop(0, trips[g], long, 0)
        lax.fori_loop(0, trips[3 + g], short, 0)

    def group(g, _):
        def score(s, count):
            for j in range(count):
                here = s + j
                row = row_tile[g, here]
                q = q_all[pl.ds(8 * jnp.minimum(row, TILES_HERE - 1), 8)].reshape(TILE, HD)
                k = kv[0, pl.ds(8 * key_tile[g, here], 8)].reshape(TILE, HD)
                dots = lax.dot_general(
                    q, k, (((1,), (1,)), ((), ())), preferred_element_type=jnp.float32
                )
                scores[here] = dots
                lanes = [dots[:, HD * n : HD * (n + 1)] for n in range(TILE // HD)]
                top = jnp.maximum(jnp.maximum(lanes[0], lanes[1]), jnp.maximum(lanes[2], lanes[3]))
                tops[row] = jnp.maximum(tops[row], top)

        walk(g, score)

        @pl.when(g == 0)
        def _():
            for c in later_copies:
                c.wait()

        for i in range(TILES_HERE):
            top = jnp.max(tops[i], axis=1, keepdims=True) * LOG2_SCALE
            tops[i] = jnp.broadcast_to(top, (TILE, HD))

        def weigh(s, count):
            for j in range(count):
                here = s + j
                row = row_tile[g, here]
                v = kv[1, pl.ds(8 * key_tile[g, here], 8)].reshape(TILE, HD)
                v = jnp.concatenate([v, jnp.ones_like(v)], axis=1)
                top = tops[row]
                weights = [
                    jnp.exp2(scores[here, :, HD * n : HD * (n + 1)] * LOG2_SCALE - top)
                    for n in range(TILE // HD)
                ]
                weights = jnp.concatenate([w.astype(jnp.bfloat16) for w in weights], axis=1)
                sums[row] += jnp.dot(weights, v, preferred_element_type=jnp.float32)

        walk(g, weigh)
        return 0

    lax.fori_loop(0, trips[2], group, 0)
    for i in range(TILES_HERE):
        result = sums[i, :, :HD] / sums[i, :, HD:]
        out[pl.ds(8 * i, 8)] = result.astype(jnp.bfloat16).reshape(8, TILE // 8, HD)


def attend(planned, q, low, own, high):
    anywhere = pl.BlockSpec(memory_space=pl.ANY)
    return pl.pallas_call(
        attention_kernel,
        grid_spec=pltpu.PrefetchScalarGridSpec(
            num_scalar_prefetch=3,
            grid=(1,),
            in_specs=[anywhere] * 4,
            out_specs=pl.BlockSpec(q.shape, lambda i, *_: (0, 0, 0)),
            scratch_shapes=[
                pltpu.VMEM(q.shape, q.dtype),
                pltpu.VMEM((2, 3 * q.shape[0]) + q.shape[1:], q.dtype),
                pltpu.VMEM((SLOTS, TILE, TILE), jnp.float32),
                pltpu.VMEM((TILES_HERE + 1, TILE, HD), jnp.float32),
                pltpu.VMEM((TILES_HERE + 1, TILE, 2 * HD), jnp.float32),
                pltpu.SemaphoreType.DMA((7,)),
            ],
        ),
        out_shape=jax.ShapeDtypeStruct(q.shape, q.dtype),
        compiler_params=pltpu.CompilerParams(vmem_limit_bytes=49 * 2**20),
        cost_estimate=pl.CostEstimate(
            flops=32 * 4 * TILE * TILE * HD, bytes_accessed=4 * 2**20, transcendentals=32 * TILE * TILE
        ),
    )(*planned, q, low, own, high)


def pack_kernel(*refs):
    ins, out = refs[:-1], refs[-1]
    for h in range(out.shape[0]):
        for a, r in enumerate(ins):
            piece = r[:, HD * h : HD * (h + 1)]
            if len(ins) > 1:
                out[h, a] = piece
            else:
                out[h] = piece


def pack(*arrays):
    rows, width = arrays[0].shape
    heads = width // HD
    steps = 2
    inner = (len(arrays), rows, HD) if len(arrays) > 1 else (rows, HD)
    nbytes = 2 * len(arrays) * rows * width * 2
    return pl.pallas_call(
        pack_kernel,
        grid=(steps,),
        in_specs=[pl.BlockSpec((rows, width // steps), lambda i: (0, i))] * len(arrays),
        out_specs=pl.BlockSpec((heads // steps,) + inner, lambda i: (i,) + (0,) * len(inner)),
        out_shape=jax.ShapeDtypeStruct((heads,) + inner, arrays[0].dtype),
        cost_estimate=pl.CostEstimate(flops=0, bytes_accessed=nbytes, transcendentals=0),
    )(*arrays)


def second_cores_turn(token, along):
    uly = lax.axis_size("uly")
    half = lax.axis_size("blk") * uly
    apart = half // 2 + uly // 2 + along // 2
    pairs = [(half + i, half + (i ^ apart)) for i in range(half)]
    return lax.ppermute(token, ("cfg", "blk", "uly"), pairs)


def exchange(x):
    return lax.all_to_all(x, "uly", split_axis=0, concat_axis=0, tiled=True)


def body(queries, key_states, value_states, tile_list, tile_used):
    blk = lax.axis_index("blk").astype(jnp.int32).reshape(1)
    count = lax.axis_size("blk")
    up = [(i, (i + 1) % count) for i in range(count)]
    down = [((i + 1) % count, i) for i in range(count)]
    turn = second_cores_turn(tile_used, TILE // queries.shape[0])
    key_states, turn = lax.optimization_barrier((key_states, turn))
    kv = exchange(pack(key_states, value_states))
    q = pack(queries)
    planned = plan(tile_list, tile_used, blk, turn)
    kv, q, planned = lax.optimization_barrier((kv, q, planned))
    low = lax.ppermute(kv, "blk", up)
    high = lax.ppermute(kv, "blk", down)
    q = exchange(q)
    out = attend(planned, q, low, kv, high)
    out = exchange(out)
    return jnp.transpose(out, (1, 0, 2)).reshape(queries.shape)


def solution(mesh):
    spec = P(("cfg", "blk", "uly"), None)
    return jax.shard_map(
        body,
        mesh=mesh,
        in_specs=(spec, spec, spec, P(), P()),
        out_specs=spec,
        check_vma=False,
    )
```
